256 devices in a mesh: group: 64 (over z, x, core), local: 4 (over y).
Axes of the slice: x: 4, y: 4, z: 8, core: 2. Of those that a mesh axis runs over, the one named last changes fastest.
Arguments:
- tokens: bfloat16 [16384, 3584], P(('group', 'local')), may hold values from -6 to 6
- expert_ids: int32 [16384, 8], P(('group', 'local')), may hold values from -1 to 127, as said below
- gate_weights: float32 [16384, 8], P(('group', 'local')), may hold values from 0.05 to 1
- w_gate: bfloat16 [3584, 131072], P(None, ('group', 'local')), may hold values from -0.09375 to 0.09375
- w_up: bfloat16 [3584, 131072], P(None, ('group', 'local')), may hold values from -0.09375 to 0.09375
- w_down: bfloat16 [131072, 3584], P(('group', 'local')), may hold values from -0.1875 to 0.1875
Outputs:
- moe_output: bfloat16 [16384, 3584], P(('group', 'local'))
The draws below stay inside these ranges and needn't reach their ends.
Inputs may be any that keep to these rules, and one draw needn't show every extreme that they name: `expert_ids`: each row names up to 8 different experts (the other entries are -1): one or two in each of at most 4 groups. At most 16 rows of one device name experts of one group, and in every draw some group is named by exactly 16 rows of every device.
All inputs are finite; a program needn't handle non-finite values.
Results may differ from the reference program's by a relative error of at most 0.012.
Values may be sent and summed in bfloat16 or wider, within the bound.
A program may use at most 128 MiB of HBM per device.

```python
import math
import jax
import jax.numpy as jnp
from jax import lax

D = 3584
FF = 1024
TOP = 8
GROUPS_TOK = 4
TOK_DEV = 64
CAP1 = 16
CAP_EXPERT = 320
GROUPS = 64
EXP_GROUP = 2
EXPERTS = 128
TOKENS = 16384
N_GROUP = 64
N_LOCAL = 4


def draw_expert_ids(key, part):
    subkeys = jax.random.split(key, 8)
    blocks = TOKENS // TOK_DEV
    hot_group = jax.random.randint(subkeys[0], (), 0, GROUPS).astype(jnp.int32)
    hot_local = jax.random.randint(subkeys[1], (), 0, EXP_GROUP).astype(jnp.int32)
    group_line = jnp.arange(GROUPS, dtype=jnp.int32)
    scores = jax.random.randint(subkeys[2], (TOKENS, GROUPS), 0, 1048576).astype(jnp.int32) * GROUPS + group_line
    scores = jnp.where(group_line == hot_group, -1, scores)
    others = lax.top_k(scores, GROUPS_TOK - 1)[1].astype(jnp.int32)
    picked = jnp.concatenate([jnp.full((TOKENS, 1), hot_group, jnp.int32), others], axis=1)
    first_local = jax.random.randint(subkeys[3], (TOKENS, GROUPS_TOK), 0, EXP_GROUP).astype(jnp.int32)
    first_local = first_local.at[:, 0].set(hot_local)
    offset = jax.random.randint(subkeys[4], (TOKENS, GROUPS_TOK), 1, EXP_GROUP).astype(jnp.int32)
    second = (first_local + offset) % EXP_GROUP
    two_named = jax.random.randint(subkeys[7], (TOKENS, GROUPS_TOK), 0, 2).astype(jnp.int32) == 1
    proposed = jnp.any(picked[:, :, None] == group_line, axis=1)
    priority = jax.random.randint(subkeys[5], (TOKENS,), 0, 1048576).astype(jnp.int32) * TOK_DEV
    priority = (priority + jnp.arange(TOKENS, dtype=jnp.int32) % TOK_DEV).reshape(blocks, TOK_DEV)
    before = (priority[:, None, :] < priority[:, :, None]).astype(jnp.int32)
    group_ranks = jnp.einsum('btu,bug->btg', before, proposed.reshape(blocks, TOK_DEV, GROUPS).astype(jnp.int32))
    kept_group = proposed & (group_ranks.reshape(TOKENS, GROUPS) < CAP1)
    kept_slot = jnp.take_along_axis(kept_group, picked, axis=1)
    first_ids = jnp.where(kept_slot, picked * EXP_GROUP + first_local, -1)
    second_ids = jnp.where(kept_slot & two_named, picked * EXP_GROUP + second, -1)
    chosen_ids = jnp.stack([first_ids, second_ids], axis=2).reshape(TOKENS, TOP)
    shuffle = jax.random.randint(subkeys[6], (TOKENS, TOP), 0, 1048576).astype(jnp.int32) * TOP + jnp.arange(TOP, dtype=jnp.int32)
    column_order = jnp.argsort(shuffle, axis=1, stable=True)
    return jnp.take_along_axis(chosen_ids, column_order, axis=1).astype(jnp.int32)


def block_levels(key, shape, cuts, smallest, largest):
    gain, own = 1.0, jax.random.fold_in(key, 6)
    for position, blocks in cuts:
        heights = jnp.exp(jax.random.uniform(jax.random.fold_in(own, position), (blocks,), jnp.float32, smallest / len(cuts), largest / len(cuts)))
        gain = gain * jnp.repeat(heights, shape[position] // blocks).reshape([-1 if axis == position else 1 for axis in range(len(shape))])
    return gain


def scatter_about(own_key, dims, deviation, most, cuts=(), kind=jnp.bfloat16):
    factor_of = block_levels(own_key, dims, cuts, -0.22, 0.18) if cuts else 1.0
    drawn = jax.random.normal(own_key, dims, jnp.float32) * deviation * factor_of
    return jnp.minimum(jnp.maximum(drawn, -most), most).astype(kind)


def setup_inputs(seed: int = 0) -> dict:
    keys = jax.random.split(jax.random.key(seed), 7)
    return {
        "tokens": scatter_about(keys[0], (TOKENS, D), 1.0, 6.0, ((0, 256),)),
        "expert_ids": draw_expert_ids(jax.random.fold_in(keys[6], 71), 0),
        "gate_weights": jnp.clip(jnp.exp(math.log(1.0) - 2.9957323 * jax.random.uniform(keys[2], (TOKENS, TOP), jnp.float32) ** block_levels(keys[2], (TOKENS, TOP), ((0, 256),), -0.2, 0.2)), 0.05, 1.0),
        "w_gate": scatter_about(keys[3], (D, EXPERTS * FF), D ** -0.5, 0.09375, ((1, 256),)),
        "w_up": scatter_about(keys[4], (D, EXPERTS * FF), D ** -0.5, 0.09375, ((1, 256),)),
        "w_down": scatter_about(keys[5], (EXPERTS * FF, D), FF ** -0.5, 0.1875, ((0, 256),)),
    }


def reference(tokens, expert_ids, gate_weights, w_gate, w_up, w_down):
    per_group = N_LOCAL // 2
    limit = N_LOCAL * CAP_EXPERT
    row_total = tokens.shape[0]
    width = tokens.shape[1]

    def expert_term(expert):
        named_here = expert_ids == expert
        chosen = jnp.any(named_here, axis=1)
        gate_row = jnp.sum(jnp.where(named_here, gate_weights, 0.0), axis=1)
        counted = chosen.astype(jnp.int32).reshape(N_GROUP, N_LOCAL, TOK_DEV)
        counted = counted.transpose(1, 0, 2).reshape(N_LOCAL, N_GROUP * TOK_DEV)
        arrive_rank = jnp.cumsum(counted, axis=1) - 1
        arrive_rank = arrive_rank.reshape(N_LOCAL, N_GROUP, TOK_DEV).transpose(1, 0, 2).reshape(row_total)
        kept_pair = chosen & (arrive_rank < CAP_EXPERT)
        row_order = jnp.argsort(1 - kept_pair.astype(jnp.int32), stable=True)[:limit].astype(jnp.int32)
        is_valid = kept_pair[row_order]
        picked_rows = tokens[row_order]
        col_start = (expert * FF).astype(jnp.int32)
        gate_cols = lax.dynamic_slice_in_dim(w_gate, col_start, FF, 1)
        up_cols = lax.dynamic_slice_in_dim(w_up, col_start, FF, 1)
        down_rows = lax.dynamic_slice_in_dim(w_down, col_start, FF, 0)
        gate_part = jnp.dot(picked_rows, gate_cols, preferred_element_type=jnp.float32)
        up_part = jnp.dot(picked_rows, up_cols, preferred_element_type=jnp.float32)
        hidden = (jax.nn.silu(gate_part) * up_part).astype(jnp.bfloat16)
        expert_out = jnp.dot(hidden, down_rows, preferred_element_type=jnp.float32)
        weighted = jnp.where(is_valid[:, None], gate_row[row_order][:, None] * expert_out, 0.0)
        return row_order, weighted.astype(jnp.bfloat16)

    def group_step(group_index, running):
        group_index = jnp.asarray(group_index).astype(jnp.int32)
        accum = jnp.zeros((row_total, width), jnp.float32)
        for slot_index in range(per_group):
            row_order, weighted = expert_term(group_index * per_group + slot_index)
            weighted = lax.optimization_barrier(weighted)
            accum = accum.at[row_order].add(weighted.astype(jnp.float32))
        group_sum = lax.optimization_barrier(accum.astype(jnp.bfloat16))
        return running + group_sum.astype(jnp.float32)

    running = lax.fori_loop(0, N_GROUP, group_step, jnp.zeros((row_total, width), jnp.float32))
    return running.astype(jnp.bfloat16)
```

```python
import jax
import jax.numpy as jnp
from jax import lax
from jax.sharding import PartitionSpec as P

N_CHUNK = 2


def shifted(array, shift):
    n_local = lax.axis_size("local")
    return lax.ppermute(array, "local", [(i, (i + shift) % n_local) for i in range(n_local)])


def one_hot_dot(select, values, spec):
    return jnp.einsum(spec, select, values, preferred_element_type=jnp.float32).astype(jnp.bfloat16)


def local(tokens, expert_ids, gate_weights, w_gate, w_up, w_down):
    n_groups = lax.axis_size("group")
    n_local = lax.axis_size("local")
    per_group = n_local // 2
    tok_rows, width = tokens.shape
    chunk = width // N_CHUNK
    send_cap = tok_rows // 4
    expert_cap = n_groups * send_cap * 5 // 16
    expert_count = n_groups * per_group
    arrived_count = n_groups * send_cap
    expert_line = jnp.arange(expert_count, dtype=jnp.int32)
    hit_table = expert_ids[:, :, None] == expert_line
    named = jnp.any(hit_table, axis=1).reshape(tok_rows, n_groups, per_group)
    gate_table = jnp.sum(jnp.where(hit_table, gate_weights[:, :, None], 0.0), axis=1)
    gate_table = gate_table.reshape(tok_rows, n_groups, per_group)
    chosen = jnp.any(named, axis=2)
    send_slot = jnp.cumsum(chosen.astype(jnp.int32), axis=0) - 1
    slot_line = jnp.arange(send_cap, dtype=jnp.int32)
    token_line = jnp.arange(tok_rows, dtype=jnp.int32)
    group_line = jnp.arange(n_groups, dtype=jnp.int32)
    match_send = chosen[:, :, None] & (send_slot[:, :, None] == slot_line)
    source_row = jnp.sum(jnp.where(match_send, token_line[:, None, None], 0), axis=0)
    send_used = jnp.any(match_send, axis=0)
    gates_out = jnp.where(send_used[:, :, None], gate_table[source_row, group_line[:, None]], 0.0)
    flags_out = (send_used[:, :, None] & named[source_row, group_line[:, None]]).astype(jnp.float32)
    meta_out = jnp.concatenate([gates_out, flags_out], axis=2)
    meta_in = lax.all_to_all(meta_out, "group", split_axis=0, concat_axis=0, tiled=True)
    meta_in = meta_in.reshape(arrived_count, 2 * per_group)
    arrived_gates = meta_in[:, :per_group]
    wanted = meta_in[:, per_group:] > 0.5
    arrive_rank = jnp.cumsum(wanted.astype(jnp.int32), axis=0) - 1
    taken = wanted & (arrive_rank < expert_cap)
    cap_line = jnp.arange(expert_cap, dtype=jnp.int32)
    match_expert = taken[:, :, None] & (arrive_rank[:, :, None] == cap_line)
    expert_gates = jnp.sum(jnp.where(match_expert, arrived_gates[:, :, None], 0.0), axis=0)
    pick = match_expert.reshape(arrived_count, per_group * expert_cap).astype(jnp.bfloat16)
    send_select = match_send.reshape(tok_rows, arrived_count).astype(jnp.bfloat16)
    here = lax.axis_index("local")
    device_line = jnp.arange(n_local, dtype=jnp.int32)

    gate_acc = None
    up_acc = None
    for c in range(N_CHUNK):
        cols = slice(c * chunk, (c + 1) * chunk)
        rows_out = one_hot_dot(send_select, tokens[:, cols], "tk,td->kd")
        rows_in = lax.all_to_all(
            rows_out.reshape(n_groups, send_cap, chunk), "group", split_axis=0, concat_axis=0, tiled=True
        ).reshape(arrived_count, chunk)
        expert_rows = one_hot_dot(pick, rows_in, "ak,ad->kd").reshape(per_group, expert_cap, chunk)
        blocks = []
        for shift in range(n_local):
            dest_expert = ((here + shift) % n_local) // 2
            block = lax.dynamic_index_in_dim(expert_rows, dest_expert, 0, keepdims=False)
            blocks.append(block if shift == 0 else shifted(block, shift))
        flat_rows = jnp.concatenate(blocks, axis=0)
        g_part = jnp.dot(flat_rows, w_gate[cols, :], preferred_element_type=jnp.float32)
        u_part = jnp.dot(flat_rows, w_up[cols, :], preferred_element_type=jnp.float32)
        gate_acc = g_part if gate_acc is None else gate_acc + g_part
        up_acc = u_part if up_acc is None else up_acc + u_part
    hidden = (jax.nn.silu(gate_acc) * up_acc).astype(jnp.bfloat16)

    outs = []
    for c in range(N_CHUNK):
        cols = slice(c * chunk, (c + 1) * chunk)
        partial_value = jnp.dot(hidden, w_down[:, cols], preferred_element_type=jnp.float32)
        partial_value = partial_value.astype(jnp.bfloat16).reshape(n_local, expert_cap, chunk)
        by_shift = [partial_value[0]] + [
            shifted(partial_value[shift], (n_local - shift) % n_local) for shift in range(1, n_local)
        ]
        back_local = jnp.take(jnp.stack(by_shift), (device_line - here) % n_local, axis=0)
        halves = back_local.astype(jnp.float32).reshape(per_group, 2, expert_cap, chunk)
        term = (expert_gates[:, :, None] * (halves[:, 0] + halves[:, 1])).astype(jnp.bfloat16)
        group_part = one_hot_dot(pick, term.reshape(per_group * expert_cap, chunk), "ak,kd->ad")
        back = lax.all_to_all(
            group_part.reshape(n_groups, send_cap, chunk), "group", split_axis=0, concat_axis=0, tiled=True
        ).reshape(arrived_count, chunk)
        outs.append(one_hot_dot(send_select, back, "tk,kd->td"))
    return jnp.concatenate(outs, axis=1)


def solution(mesh):
    in_specs = (
        P(("group", "local"), None),
        P(("group", "local"), None),
        P(("group", "local"), None),
        P(None, ("group", "local")),
        P(None, ("group", "local")),
        P(("group", "local"), None),
    )
    out_specs = P(("group", "local"), None)
    return jax.shard_map(local, mesh=mesh, in_specs=in_specs, out_specs=out_specs, check_vma=False)
```

```python
import jax
import jax.numpy as jnp
from jax import lax
from jax.sharding import PartitionSpec as P

N_CHUNK = 2


def shifted(array, shift):
    n_local = lax.axis_size("local")
    return lax.ppermute(array, "local", [(i, (i + shift) % n_local) for i in range(n_local)])


def one_hot_dot(select, values, spec):
    return jnp.einsum(spec, select, values, preferred_element_type=jnp.float32).astype(jnp.bfloat16)


def local(tokens, expert_ids, gate_weights, w_gate, w_up, w_down):
    n_groups = lax.axis_size("group")
    n_local = lax.axis_size("local")
    per_group = n_local // 2
    tok_rows, width = tokens.shape
    chunk = width // N_CHUNK
    send_cap = tok_rows // 4
    expert_cap = n_groups * send_cap * 5 // 16
    expert_count = n_groups * per_group
    arrived_count = n_groups * send_cap
    expert_line = jnp.arange(expert_count, dtype=jnp.int32)
    hit_table = expert_ids[:, :, None] == expert_line
    named = jnp.any(hit_table, axis=1).reshape(tok_rows, n_groups, per_group)
    gate_table = jnp.sum(jnp.where(hit_table, gate_weights[:, :, None], 0.0), axis=1)
    gate_table = gate_table.reshape(tok_rows, n_groups, per_group)
    chosen = jnp.any(named, axis=2)
    send_slot = jnp.cumsum(chosen.astype(jnp.int32), axis=0) - 1
    slot_line = jnp.arange(send_cap, dtype=jnp.int32)
    token_line = jnp.arange(tok_rows, dtype=jnp.int32)
    group_line = jnp.arange(n_groups, dtype=jnp.int32)
    match_send = chosen[:, :, None] & (send_slot[:, :, None] == slot_line)
    source_row = jnp.sum(jnp.where(match_send, token_line[:, None, None], 0), axis=0)
    send_used = jnp.any(match_send, axis=0)
    gates_out = jnp.where(send_used[:, :, None], gate_table[source_row, group_line[:, None]], 0.0)
    flags_out = (send_used[:, :, None] & named[source_row, group_line[:, None]]).astype(jnp.float32)
    meta_out = jnp.concatenate([gates_out, flags_out], axis=2)
    meta_in = lax.all_to_all(meta_out, "group", split_axis=0, concat_axis=0, tiled=True)
    meta_in = meta_in.reshape(arrived_count, 2 * per_group)
    arrived_gates = meta_in[:, :per_group]
    wanted = meta_in[:, per_group:] > 0.5
    arrive_rank = jnp.cumsum(wanted.astype(jnp.int32), axis=0) - 1
    taken = wanted & (arrive_rank < expert_cap)
    cap_line = jnp.arange(expert_cap, dtype=jnp.int32)
    match_expert = taken[:, :, None] & (arrive_rank[:, :, None] == cap_line)
    expert_gates = jnp.sum(jnp.where(match_expert, arrived_gates[:, :, None], 0.0), axis=0)
    pick = match_expert.reshape(arrived_count, per_group * expert_cap).astype(jnp.bfloat16)
    send_select = match_send.reshape(tok_rows, arrived_count).astype(jnp.bfloat16)
    here = lax.axis_index("local")
    device_line = jnp.arange(n_local, dtype=jnp.int32)

    gate_acc = None
    up_acc = None
    for c in range(N_CHUNK):
        cols = slice(c * chunk, (c + 1) * chunk)
        rows_out = one_hot_dot(send_select, tokens[:, cols], "tk,td->kd")
        rows_in = lax.all_to_all(
            rows_out.reshape(n_groups, send_cap, chunk), "group", split_axis=0, concat_axis=0, tiled=True
        ).reshape(arrived_count, chunk)
        expert_rows = one_hot_dot(pick, rows_in, "ak,ad->kd").reshape(per_group, expert_cap, chunk)
        blocks = []
        for shift in range(n_local):
            dest_expert = ((here + shift) % n_local) // 2
            block = lax.dynamic_index_in_dim(expert_rows, dest_expert, 0, keepdims=False)
            blocks.append(block if shift == 0 else shifted(block, shift))
        flat_rows = jnp.concatenate(blocks, axis=0)
        g_part = jnp.dot(flat_rows, w_gate[cols, :], preferred_element_type=jnp.float32)
        u_part = jnp.dot(flat_rows, w_up[cols, :], preferred_element_type=jnp.float32)
        gate_acc = g_part if gate_acc is None else gate_acc + g_part
        up_acc = u_part if up_acc is None else up_acc + u_part
    hidden = (jax.nn.silu(gate_acc) * up_acc).astype(jnp.bfloat16)

    outs = []
    owner = ((here + device_line) % n_local) // 2 == jnp.arange(per_group, dtype=jnp.int32)[:, None]
    for c in range(N_CHUNK):
        cols = slice(c * chunk, (c + 1) * chunk)
        partial_value = jnp.dot(hidden, w_down[:, cols], preferred_element_type=jnp.float32)
        partial_value = partial_value.astype(jnp.bfloat16).reshape(n_local, expert_cap, chunk)
        by_shift = [partial_value[0]] + [
            shifted(partial_value[shift], (n_local - shift) % n_local) for shift in range(1, n_local)
        ]
        stacked, owner_c, gates_c, pick_c = lax.optimization_barrier((jnp.stack(by_shift), owner, expert_gates, pick))
        summed = jnp.sum(jnp.where(owner_c[:, :, None, None], stacked.astype(jnp.float32)[None], 0.0), axis=1)
        term = (gates_c[:, :, None] * summed).astype(jnp.bfloat16)
        group_part = one_hot_dot(pick_c, term.reshape(per_group * expert_cap, chunk), "ak,kd->ad")
        back = lax.all_to_all(
            group_part.reshape(n_groups, send_cap, chunk), "group", split_axis=0, concat_axis=0, tiled=True
        ).reshape(arrived_count, chunk)
        outs.append(one_hot_dot(send_select, back, "tk,kd->td"))
    return jnp.concatenate(outs, axis=1)


def solution(mesh):
    in_specs = (
        P(("group", "local"), None),
        P(("group", "local"), None),
        P(("group", "local"), None),
        P(None, ("group", "local")),
        P(None, ("group", "local")),
        P(("group", "local"), None),
    )
    out_specs = P(("group", "local"), None)

    return jax.shard_map(local, mesh=mesh, in_specs=in_specs, out_specs=out_specs, check_vma=False)
```

```python
import jax
import jax.numpy as jnp
from jax import lax
from jax.sharding import PartitionSpec as P

N_CHUNK = 4


def shifted(array, shift):
    n_local = lax.axis_size("local")
    return lax.ppermute(array, "local", [(i, (i + shift) % n_local) for i in range(n_local)])


def one_hot_dot(select, values, spec):
    return jnp.einsum(spec, select, values, preferred_element_type=jnp.float32).astype(jnp.bfloat16)


def local(tokens, expert_ids, gate_weights, w_gate, w_up, w_down):
    n_groups = lax.axis_size("group")
    n_local = lax.axis_size("local")
    per_group = n_local // 2
    tok_rows, width = tokens.shape
    chunk = width // N_CHUNK
    send_cap = tok_rows // 4
    expert_cap = n_groups * send_cap * 5 // 16
    expert_count = n_groups * per_group
    arrived_count = n_groups * send_cap
    expert_line = jnp.arange(expert_count, dtype=jnp.int32)
    hit_table = expert_ids[:, :, None] == expert_line
    named = jnp.any(hit_table, axis=1).reshape(tok_rows, n_groups, per_group)
    gate_table = jnp.sum(jnp.where(hit_table, gate_weights[:, :, None], 0.0), axis=1)
    gate_table = gate_table.reshape(tok_rows, n_groups, per_group)
    chosen = jnp.any(named, axis=2)
    send_slot = jnp.cumsum(chosen.astype(jnp.int32), axis=0) - 1
    slot_line = jnp.arange(send_cap, dtype=jnp.int32)
    token_line = jnp.arange(tok_rows, dtype=jnp.int32)
    group_line = jnp.arange(n_groups, dtype=jnp.int32)
    match_send = chosen[:, :, None] & (send_slot[:, :, None] == slot_line)
    source_row = jnp.sum(jnp.where(match_send, token_line[:, None, None], 0), axis=0)
    send_used = jnp.any(match_send, axis=0)
    gates_out = jnp.sum(jnp.where(match_send[:, :, :, None], gate_table[:, :, None, :], 0.0), axis=0)
    flags_out = jnp.any(match_send[:, :, :, None] & named[:, :, None, :], axis=0).astype(jnp.bfloat16)
    gates_hi = gates_out.astype(jnp.bfloat16)
    gates_lo = (gates_out - gates_hi.astype(jnp.float32)).astype(jnp.bfloat16)
    meta_out = jnp.concatenate([gates_hi, gates_lo, flags_out], axis=2)
    meta_width = 128
    meta_out = jnp.pad(meta_out, ((0, 0), (0, 0), (0, meta_width - 3 * per_group)))

    def route(meta_in):
        meta_in = meta_in.reshape(arrived_count, meta_width)[:, : 3 * per_group].astype(jnp.float32)
        arrived_gates = meta_in[:, :per_group] + meta_in[:, per_group : 2 * per_group]
        wanted = meta_in[:, 2 * per_group :] > 0.5
        arrive_rank = jnp.cumsum(wanted.astype(jnp.int32), axis=0) - 1
        taken = wanted & (arrive_rank < expert_cap)
        cap_line = jnp.arange(expert_cap, dtype=jnp.int32)
        match_expert = taken[:, :, None] & (arrive_rank[:, :, None] == cap_line)
        expert_gates = jnp.sum(jnp.where(match_expert, arrived_gates[:, :, None], 0.0), axis=0)
        pick = match_expert.reshape(arrived_count, per_group * expert_cap).astype(jnp.bfloat16)
        return expert_gates, pick

    send_select = match_send.reshape(tok_rows, arrived_count).astype(jnp.bfloat16)
    here = lax.axis_index("local")
    device_line = jnp.arange(n_local, dtype=jnp.int32)

    gate_acc = None
    up_acc = None
    for c in range(N_CHUNK):
        cols = slice(c * chunk, (c + 1) * chunk)
        rows_out = one_hot_dot(send_select, tokens[:, cols], "tk,td->kd")
        rows_out = rows_out.reshape(n_groups, send_cap, chunk)
        if c == 0:
            rows_out = jnp.concatenate([rows_out, meta_out], axis=2)
        rows_in = lax.all_to_all(rows_out, "group", split_axis=0, concat_axis=0, tiled=True)
        if c == 0:
            expert_gates, pick = route(rows_in[:, :, chunk:])
        rows_in = rows_in[:, :, :chunk].reshape(arrived_count, chunk)
        expert_rows = one_hot_dot(pick, rows_in, "ak,ad->kd").reshape(per_group, expert_cap, chunk)
        blocks = []
        for shift in range(n_local):
            dest_expert = ((here + shift) % n_local) // 2
            block = lax.dynamic_index_in_dim(expert_rows, dest_expert, 0, keepdims=False)
            blocks.append(block if shift == 0 else shifted(block, shift))
        flat_rows = jnp.concatenate(blocks, axis=0)
        g_part = jnp.dot(flat_rows, w_gate[cols, :], preferred_element_type=jnp.float32)
        u_part = jnp.dot(flat_rows, w_up[cols, :], preferred_element_type=jnp.float32)
        gate_acc = g_part if gate_acc is None else gate_acc + g_part
        up_acc = u_part if up_acc is None else up_acc + u_part
    hidden = (jax.nn.silu(gate_acc) * up_acc).astype(jnp.bfloat16)

    outs = []
    owner = ((here + device_line) % n_local) // 2 == jnp.arange(per_group, dtype=jnp.int32)[:, None]
    for c in range(N_CHUNK):
        cols = slice(c * chunk, (c + 1) * chunk)
        partial_value = jnp.dot(hidden, w_down[:, cols], preferred_element_type=jnp.float32)
        partial_value = partial_value.astype(jnp.bfloat16).reshape(n_local, expert_cap, chunk)
        by_shift = [partial_value[0]] + [
            shifted(partial_value[shift], (n_local - shift) % n_local) for shift in range(1, n_local)
        ]
        stacked, owner_c, gates_c, pick_c = lax.optimization_barrier((jnp.stack(by_shift), owner, expert_gates, pick))
        summed = jnp.sum(jnp.where(owner_c[:, :, None, None], stacked.astype(jnp.float32)[None], 0.0), axis=1)
        term = (gates_c[:, :, None] * summed).astype(jnp.bfloat16)
        group_part = one_hot_dot(pick_c, term.reshape(per_group * expert_cap, chunk), "ak,kd->ad")
        back = lax.all_to_all(
            group_part.reshape(n_groups, send_cap, chunk), "group", split_axis=0, concat_axis=0, tiled=True
        ).reshape(arrived_count, chunk)
        outs.append(one_hot_dot(send_select, back, "tk,kd->td"))
    return jnp.concatenate(outs, axis=1)


def solution(mesh):
    in_specs = (
        P(("group", "local"), None),
        P(("group", "local"), None),
        P(("group", "local"), None),
        P(None, ("group", "local")),
        P(None, ("group", "local")),
        P(("group", "local"), None),
    )
    out_specs = P(("group", "local"), None)

    return jax.shard_map(local, mesh=mesh, in_specs=in_specs, out_specs=out_specs, check_vma=False)
```

```python
import jax
import jax.numpy as jnp
from jax import lax
from jax.sharding import PartitionSpec as P

GO_UNITS = (10, 8, 6, 4)
RET_UNITS = (4, 6, 8, 10)


def bounds(units, width):
    step = width // sum(units)
    edges = [0]
    for unit in units:
        edges.append(edges[-1] + unit * step)
    return [slice(a, b) for a, b in zip(edges[:-1], edges[1:])]


def shifted(array, shift):
    n_local = lax.axis_size("local")
    return lax.ppermute(array, "local", [(i, (i + shift) % n_local) for i in range(n_local)])


def one_hot_dot(select, values, spec):
    return jnp.einsum(spec, select, values, preferred_element_type=jnp.float32).astype(jnp.bfloat16)


def local(tokens, expert_ids, gate_weights, w_gate, w_up, w_down):
    n_groups = lax.axis_size("group")
    n_local = lax.axis_size("local")
    per_group = n_local // 2
    tok_rows, width = tokens.shape
    send_cap = tok_rows // 4
    expert_cap = n_groups * send_cap * 5 // 16
    expert_count = n_groups * per_group
    arrived_count = n_groups * send_cap
    expert_line = jnp.arange(expert_count, dtype=jnp.int32)
    hit_table = expert_ids[:, :, None] == expert_line
    named = jnp.any(hit_table, axis=1).reshape(tok_rows, n_groups, per_group)
    gate_table = jnp.sum(jnp.where(hit_table, gate_weights[:, :, None], 0.0), axis=1)
    gate_table = gate_table.reshape(tok_rows, n_groups, per_group)
    chosen = jnp.any(named, axis=2)
    send_slot = jnp.cumsum(chosen.astype(jnp.int32), axis=0) - 1
    slot_line = jnp.arange(send_cap, dtype=jnp.int32)
    token_line = jnp.arange(tok_rows, dtype=jnp.int32)
    group_line = jnp.arange(n_groups, dtype=jnp.int32)
    match_send = chosen[:, :, None] & (send_slot[:, :, None] == slot_line)
    source_row = jnp.sum(jnp.where(match_send, token_line[:, None, None], 0), axis=0)
    send_used = jnp.any(match_send, axis=0)
    gates_out = jnp.sum(jnp.where(match_send[:, :, :, None], gate_table[:, :, None, :], 0.0), axis=0)
    flags_out = jnp.any(match_send[:, :, :, None] & named[:, :, None, :], axis=0).astype(jnp.bfloat16)
    gates_hi = gates_out.astype(jnp.bfloat16)
    gates_lo = (gates_out - gates_hi.astype(jnp.float32)).astype(jnp.bfloat16)
    meta_out = jnp.concatenate([gates_hi, gates_lo, flags_out], axis=2)
    meta_width = 128
    meta_out = jnp.pad(meta_out, ((0, 0), (0, 0), (0, meta_width - 3 * per_group)))

    def route(meta_in):
        meta_in = meta_in.reshape(arrived_count, meta_width)[:, : 3 * per_group].astype(jnp.float32)
        arrived_gates = meta_in[:, :per_group] + meta_in[:, per_group : 2 * per_group]
        wanted = meta_in[:, 2 * per_group :] > 0.5
        arrive_rank = jnp.cumsum(wanted.astype(jnp.int32), axis=0) - 1
        taken = wanted & (arrive_rank < expert_cap)
        cap_line = jnp.arange(expert_cap, dtype=jnp.int32)
        match_expert = taken[:, :, None] & (arrive_rank[:, :, None] == cap_line)
        expert_gates = jnp.sum(jnp.where(match_expert, arrived_gates[:, :, None], 0.0), axis=0)
        pick = match_expert.reshape(arrived_count, per_group * expert_cap).astype(jnp.bfloat16)
        return expert_gates, pick

    send_select = match_send.reshape(tok_rows, arrived_count).astype(jnp.bfloat16)
    here = lax.axis_index("local")
    device_line = jnp.arange(n_local, dtype=jnp.int32)

    gate_acc = None
    up_acc = None
    for c, cols in enumerate(bounds(GO_UNITS, width)):
        chunk = cols.stop - cols.start
        rows_out = one_hot_dot(send_select, tokens[:, cols], "tk,td->kd")
        rows_out = rows_out.reshape(n_groups, send_cap, chunk)
        if c == 0:
            rows_out = jnp.concatenate([rows_out, meta_out], axis=2)
        rows_in = lax.all_to_all(rows_out, "group", split_axis=0, concat_axis=0, tiled=True)
        if c == 0:
            expert_gates, pick = route(rows_in[:, :, chunk:])
        rows_in = rows_in[:, :, :chunk].reshape(arrived_count, chunk)
        expert_rows = one_hot_dot(pick, rows_in, "ak,ad->kd").reshape(per_group, expert_cap, chunk)
        blocks = []
        for shift in range(n_local):
            dest_expert = ((here + shift) % n_local) // 2
            block = lax.dynamic_index_in_dim(expert_rows, dest_expert, 0, keepdims=False)
            blocks.append(block if shift == 0 else shifted(block, shift))
        flat_rows = jnp.concatenate(blocks, axis=0)
        g_part = jnp.dot(flat_rows, w_gate[cols, :], preferred_element_type=jnp.float32)
        u_part = jnp.dot(flat_rows, w_up[cols, :], preferred_element_type=jnp.float32)
        gate_acc = g_part if gate_acc is None else gate_acc + g_part
        up_acc = u_part if up_acc is None else up_acc + u_part
    hidden = (jax.nn.silu(gate_acc) * up_acc).astype(jnp.bfloat16)

    outs = []
    owner = ((here + device_line) % n_local) // 2 == jnp.arange(per_group, dtype=jnp.int32)[:, None]
    for cols in bounds(RET_UNITS, width):
        chunk = cols.stop - cols.start
        partial_value = jnp.dot(hidden, w_down[:, cols], preferred_element_type=jnp.float32)
        partial_value = partial_value.astype(jnp.bfloat16).reshape(n_local, expert_cap, chunk)
        by_shift = [partial_value[0]] + [
            shifted(partial_value[shift], (n_local - shift) % n_local) for shift in range(1, n_local)
        ]
        stacked, owner_c, gates_c, pick_c = lax.optimization_barrier((jnp.stack(by_shift), owner, expert_gates, pick))
        summed = jnp.sum(jnp.where(owner_c[:, :, None, None], stacked.astype(jnp.float32)[None], 0.0), axis=1)
        term = (gates_c[:, :, None] * summed).astype(jnp.bfloat16)
        group_part = one_hot_dot(pick_c, term.reshape(per_group * expert_cap, chunk), "ak,kd->ad")
        back = lax.all_to_all(
            group_part.reshape(n_groups, send_cap, chunk), "group", split_axis=0, concat_axis=0, tiled=True
        ).reshape(arrived_count, chunk)
        outs.append(one_hot_dot(send_select, back, "tk,kd->td"))
    return jnp.concatenate(outs, axis=1)


def solution(mesh):
    in_specs = (
        P(("group", "local"), None),
        P(("group", "local"), None),
        P(("group", "local"), None),
        P(None, ("group", "local")),
        P(None, ("group", "local")),
        P(("group", "local"), None),
    )
    out_specs = P(("group", "local"), None)

    return jax.shard_map(local, mesh=mesh, in_specs=in_specs, out_specs=out_specs, check_vma=False)
```

```python
import jax
import jax.numpy as jnp
from jax import lax
from jax.sharding import PartitionSpec as P

GO_UNITS = (12, 12, 4)
RET_UNITS = (4, 8, 8, 8)


def bounds(units, width):
    step = width // sum(units)
    edges = [0]
    for unit in units:
        edges.append(edges[-1] + unit * step)
    return [slice(a, b) for a, b in zip(edges[:-1], edges[1:])]


def shifted(array, shift):
    n_local = lax.axis_size("local")
    return lax.ppermute(array, "local", [(i, (i + shift) % n_local) for i in range(n_local)])


def one_hot_dot(select, values, spec):
    return jnp.einsum(spec, select, values, preferred_element_type=jnp.float32).astype(jnp.bfloat16)


def local(tokens, expert_ids, gate_weights, w_gate, w_up, w_down):
    n_groups = lax.axis_size("group")
    n_local = lax.axis_size("local")
    per_group = n_local // 2
    tok_rows, width = tokens.shape
    send_cap = tok_rows // 4
    expert_cap = n_groups * send_cap * 5 // 16
    expert_count = n_groups * per_group
    arrived_count = n_groups * send_cap
    expert_line = jnp.arange(expert_count, dtype=jnp.int32)
    hit_table = expert_ids[:, :, None] == expert_line
    named = jnp.any(hit_table, axis=1).reshape(tok_rows, n_groups, per_group)
    gate_table = jnp.sum(jnp.where(hit_table, gate_weights[:, :, None], 0.0), axis=1)
    gate_table = gate_table.reshape(tok_rows, n_groups, per_group)
    chosen = jnp.any(named, axis=2)
    send_slot = jnp.cumsum(chosen.astype(jnp.int32), axis=0) - 1
    slot_line = jnp.arange(send_cap, dtype=jnp.int32)
    token_line = jnp.arange(tok_rows, dtype=jnp.int32)
    group_line = jnp.arange(n_groups, dtype=jnp.int32)
    match_send = chosen[:, :, None] & (send_slot[:, :, None] == slot_line)
    source_row = jnp.sum(jnp.where(match_send, token_line[:, None, None], 0), axis=0)
    send_used = jnp.any(match_send, axis=0)
    gates_out = jnp.sum(jnp.where(match_send[:, :, :, None], gate_table[:, :, None, :], 0.0), axis=0)
    flags_out = jnp.any(match_send[:, :, :, None] & named[:, :, None, :], axis=0).astype(jnp.bfloat16)
    gates_hi = gates_out.astype(jnp.bfloat16)
    gates_lo = (gates_out - gates_hi.astype(jnp.float32)).astype(jnp.bfloat16)
    meta_out = jnp.concatenate([gates_hi, gates_lo, flags_out], axis=2)
    meta_width = 128
    meta_out = jnp.pad(meta_out, ((0, 0), (0, 0), (0, meta_width - 3 * per_group)))

    def route(meta_in):
        meta_in = meta_in.reshape(arrived_count, meta_width)[:, : 3 * per_group].astype(jnp.float32)
        arrived_gates = meta_in[:, :per_group] + meta_in[:, per_group : 2 * per_group]
        wanted = meta_in[:, 2 * per_group :] > 0.5
        arrive_rank = jnp.cumsum(wanted.astype(jnp.int32), axis=0) - 1
        taken = wanted & (arrive_rank < expert_cap)
        cap_line = jnp.arange(expert_cap, dtype=jnp.int32)
        match_expert = taken[:, :, None] & (arrive_rank[:, :, None] == cap_line)
        expert_gates = jnp.sum(jnp.where(match_expert, arrived_gates[:, :, None], 0.0), axis=0)
        pick = match_expert.reshape(arrived_count, per_group * expert_cap).astype(jnp.bfloat16)
        return expert_gates, pick

    send_select = match_send.reshape(tok_rows, arrived_count).astype(jnp.bfloat16)
    here = lax.axis_index("local")
    device_line = jnp.arange(n_local, dtype=jnp.int32)

    gate_acc = None
    up_acc = None
    for c, cols in enumerate(bounds(GO_UNITS, width)):
        chunk = cols.stop - cols.start
        rows_out = one_hot_dot(send_select, tokens[:, cols], "tk,td->kd")
        rows_out = rows_out.reshape(n_groups, send_cap, chunk)
        if c == 0:
            rows_out = jnp.concatenate([rows_out, meta_out], axis=2)
        rows_in = lax.all_to_all(rows_out, "group", split_axis=0, concat_axis=0, tiled=True)
        if c == 0:
            expert_gates, pick = route(rows_in[:, :, chunk:])
        rows_in = rows_in[:, :, :chunk].reshape(arrived_count, chunk)
        expert_rows = one_hot_dot(pick, rows_in, "ak,ad->kd").reshape(per_group, expert_cap, chunk)
        blocks = []
        for shift in range(n_local):
            dest_expert = ((here + shift) % n_local) // 2
            block = lax.dynamic_index_in_dim(expert_rows, dest_expert, 0, keepdims=False)
            blocks.append(block if shift == 0 else shifted(block, shift))
        flat_rows = jnp.concatenate(blocks, axis=0)
        g_part = jnp.dot(flat_rows, w_gate[cols, :], preferred_element_type=jnp.float32)
        u_part = jnp.dot(flat_rows, w_up[cols, :], preferred_element_type=jnp.float32)
        gate_acc = g_part if gate_acc is None else gate_acc + g_part
        up_acc = u_part if up_acc is None else up_acc + u_part
    hidden = (jax.nn.silu(gate_acc) * up_acc).astype(jnp.bfloat16)

    outs = []
    owner = ((here + device_line) % n_local) // 2 == jnp.arange(per_group, dtype=jnp.int32)[:, None]
    gated = pick.reshape(arrived_count, per_group, expert_cap) * expert_gates.astype(jnp.bfloat16)[None]
    comb = jnp.concatenate(
        [jnp.sum(jnp.where(owner[None, :, j, None], gated, 0.0), axis=1) for j in range(n_local)], axis=1
    ).astype(jnp.bfloat16)
    for cols in bounds(RET_UNITS, width):
        chunk = cols.stop - cols.start
        partial_value = jnp.dot(hidden, w_down[:, cols], preferred_element_type=jnp.float32)
        partial_value = partial_value.astype(jnp.bfloat16).reshape(n_local, expert_cap, chunk)
        by_shift = [partial_value[0]] + [
            shifted(partial_value[shift], (n_local - shift) % n_local) for shift in range(1, n_local)
        ]
        stacked, comb_c = lax.optimization_barrier((jnp.concatenate(by_shift, axis=0), comb))
        group_part = one_hot_dot(comb_c, stacked, "ak,kd->ad")
        back = lax.all_to_all(
            group_part.reshape(n_groups, send_cap, chunk), "group", split_axis=0, concat_axis=0, tiled=True
        ).reshape(arrived_count, chunk)
        outs.append(one_hot_dot(send_select, back, "tk,kd->td"))
    return jnp.concatenate(outs, axis=1)


def solution(mesh):
    in_specs = (
        P(("group", "local"), None),
        P(("group", "local"), None),
        P(("group", "local"), None),
        P(None, ("group", "local")),
        P(None, ("group", "local")),
        P(("group", "local"), None),
    )
    out_specs = P(("group", "local"), None)

    return jax.shard_map(local, mesh=mesh, in_specs=in_specs, out_specs=out_specs, check_vma=False)
```

```python
import jax
import jax.numpy as jnp
from jax import lax
from jax.sharding import PartitionSpec as P

GO_UNITS = (8, 8, 8, 4)
RET_UNITS = (4, 8, 8, 8)


def bounds(units, width):
    step = width // sum(units)
    edges = [0]
    for unit in units:
        edges.append(edges[-1] + unit * step)
    return [slice(a, b) for a, b in zip(edges[:-1], edges[1:])]


def shifted(array, shift):
    n_local = lax.axis_size("local")
    return lax.ppermute(array, "local", [(i, (i + shift) % n_local) for i in range(n_local)])


def one_hot_dot(select, values, spec):
    return jnp.einsum(spec, select, values, preferred_element_type=jnp.float32).astype(jnp.bfloat16)


def local(tokens, expert_ids, gate_weights, w_gate, w_up, w_down):
    n_groups = lax.axis_size("group")
    n_local = lax.axis_size("local")
    per_group = n_local // 2
    tok_rows, width = tokens.shape
    send_cap = tok_rows // 4
    expert_cap = n_groups * send_cap * 5 // 16
    expert_count = n_groups * per_group
    arrived_count = n_groups * send_cap
    expert_line = jnp.arange(expert_count, dtype=jnp.int32)
    hit_table = expert_ids[:, :, None] == expert_line
    named = jnp.any(hit_table, axis=1).reshape(tok_rows, n_groups, per_group)
    gate_table = jnp.sum(jnp.where(hit_table, gate_weights[:, :, None], 0.0), axis=1)
    gate_table = gate_table.reshape(tok_rows, n_groups, per_group)
    chosen = jnp.any(named, axis=2)
    send_slot = jnp.cumsum(chosen.astype(jnp.int32), axis=0) - 1
    slot_line = jnp.arange(send_cap, dtype=jnp.int32)
    token_line = jnp.arange(tok_rows, dtype=jnp.int32)
    group_line = jnp.arange(n_groups, dtype=jnp.int32)
    match_send = chosen[:, :, None] & (send_slot[:, :, None] == slot_line)
    source_row = jnp.sum(jnp.where(match_send, token_line[:, None, None], 0), axis=0)
    send_used = jnp.any(match_send, axis=0)
    gates_out = jnp.sum(jnp.where(match_send[:, :, :, None], gate_table[:, :, None, :], 0.0), axis=0)
    flags_out = jnp.any(match_send[:, :, :, None] & named[:, :, None, :], axis=0).astype(jnp.bfloat16)
    gates_hi = gates_out.astype(jnp.bfloat16)
    gates_lo = (gates_out - gates_hi.astype(jnp.float32)).astype(jnp.bfloat16)
    meta_out = jnp.concatenate([gates_hi, gates_lo, flags_out], axis=2)
    meta_width = 128
    meta_out = jnp.pad(meta_out, ((0, 0), (0, 0), (0, meta_width - 3 * per_group)))

    def route(meta_in):
        meta_in = meta_in.reshape(arrived_count, meta_width)[:, : 3 * per_group].astype(jnp.float32)
        arrived_gates = meta_in[:, :per_group] + meta_in[:, per_group : 2 * per_group]
        wanted = meta_in[:, 2 * per_group :] > 0.5
        arrive_rank = jnp.cumsum(wanted.astype(jnp.int32), axis=0) - 1
        taken = wanted & (arrive_rank < expert_cap)
        cap_line = jnp.arange(expert_cap, dtype=jnp.int32)
        match_expert = taken[:, :, None] & (arrive_rank[:, :, None] == cap_line)
        expert_gates = jnp.sum(jnp.where(match_expert, arrived_gates[:, :, None], 0.0), axis=0)
        pick = match_expert.reshape(arrived_count, per_group * expert_cap).astype(jnp.bfloat16)
        return expert_gates, pick

    send_select = match_send.reshape(tok_rows, arrived_count).astype(jnp.bfloat16)
    here = lax.axis_index("local")
    device_line = jnp.arange(n_local, dtype=jnp.int32)

    gate_acc = None
    up_acc = None
    for c, cols in enumerate(bounds(GO_UNITS, width)):
        chunk = cols.stop - cols.start
        rows_out = one_hot_dot(send_select, tokens[:, cols], "tk,td->kd")
        rows_out = rows_out.reshape(n_groups, send_cap, chunk)
        if c == 0:
            rows_out = jnp.concatenate([rows_out, meta_out], axis=2)
        rows_in = lax.all_to_all(rows_out, "group", split_axis=0, concat_axis=0, tiled=True)
        if c == 0:
            expert_gates, pick = route(rows_in[:, :, chunk:])
        rows_in = rows_in[:, :, :chunk].reshape(arrived_count, chunk)
        if c == 0:
            owner = ((here + device_line) % n_local) // 2 == jnp.arange(per_group, dtype=jnp.int32)[:, None]
            pick3 = pick.reshape(arrived_count, per_group, expert_cap)
            by_dest = jnp.concatenate(
                [jnp.sum(jnp.where(owner[None, :, j, None], pick3, 0.0), axis=1) for j in range(n_local)],
                axis=1,
            ).astype(jnp.bfloat16)
        dest_rows = one_hot_dot(by_dest, rows_in, "ak,ad->kd").reshape(n_local, expert_cap, chunk)
        blocks = []
        for shift in range(n_local):
            block = dest_rows[shift]
            blocks.append(block if shift == 0 else shifted(block, shift))
        flat_rows = jnp.concatenate(blocks, axis=0)
        g_part = jnp.dot(flat_rows, w_gate[cols, :], preferred_element_type=jnp.float32)
        u_part = jnp.dot(flat_rows, w_up[cols, :], preferred_element_type=jnp.float32)
        gate_acc = g_part if gate_acc is None else gate_acc + g_part
        up_acc = u_part if up_acc is None else up_acc + u_part
    hidden = (jax.nn.silu(gate_acc) * up_acc).astype(jnp.bfloat16)

    outs = []
    owner = ((here + device_line) % n_local) // 2 == jnp.arange(per_group, dtype=jnp.int32)[:, None]
    gated = pick.reshape(arrived_count, per_group, expert_cap) * expert_gates.astype(jnp.bfloat16)[None]
    comb = jnp.concatenate(
        [jnp.sum(jnp.where(owner[None, :, j, None], gated, 0.0), axis=1) for j in range(n_local)], axis=1
    ).astype(jnp.bfloat16)
    for cols in bounds(RET_UNITS, width):
        chunk = cols.stop - cols.start
        partial_value = jnp.dot(hidden, w_down[:, cols], preferred_element_type=jnp.float32)
        partial_value = partial_value.astype(jnp.bfloat16).reshape(n_local, expert_cap, chunk)
        by_shift = [partial_value[0]] + [
            shifted(partial_value[shift], (n_local - shift) % n_local) for shift in range(1, n_local)
        ]
        stacked, comb_c = lax.optimization_barrier((jnp.concatenate(by_shift, axis=0), comb))
        group_part = one_hot_dot(comb_c, stacked, "ak,kd->ad")
        back = lax.all_to_all(
            group_part.reshape(n_groups, send_cap, chunk), "group", split_axis=0, concat_axis=0, tiled=True
        ).reshape(arrived_count, chunk)
        outs.append(one_hot_dot(send_select, back, "tk,kd->td"))
    return jnp.concatenate(outs, axis=1)


def solution(mesh):
    in_specs = (
        P(("group", "local"), None),
        P(("group", "local"), None),
        P(("group", "local"), None),
        P(None, ("group", "local")),
        P(None, ("group", "local")),
        P(("group", "local"), None),
    )
    out_specs = P(("group", "local"), None)

    return jax.shard_map(local, mesh=mesh, in_specs=in_specs, out_specs=out_specs, check_vma=False)
```
